32 devices in a mesh: batch: 8 (over z, x), seq: 4 (over y, core).
Axes of the slice: x: 2, y: 2, z: 4, core: 2. Of those that a mesh axis runs over, the one named last changes fastest.
Arguments:
- hidden: bfloat16 [8, 2048, 1536], P('batch', 'seq'), may hold values from -6 to 6
- in_proj: bfloat16 [1536, 6448], P(('batch', 'seq')), may hold values from -1 to 1
- out_proj: bfloat16 [3072, 1536], P(('batch', 'seq')), may hold values from -0.109375 to 0.109375
- conv_weight: bfloat16 [4, 3328], P(None, ('batch', 'seq')), may hold values from -3 to 3
- conv_bias: bfloat16 [3328], P(('batch', 'seq')), may hold values from -1.5 to 1.5
- step_bias: float32 [48], replicated, may hold values from -10 to -3
- decay_log: float32 [48], replicated, may hold values from -1.2 to 0.7
- skip_weight: float32 [48], replicated, may hold values from 0.2 to 1.5
- gated_gain: bfloat16 [3072], P(('batch', 'seq')), may hold values from 0.5 to 1.5
- norm_gain: bfloat16 [1536], P(('batch', 'seq')), may hold values from 0.5 to 1.5
- cotangent: bfloat16 [8, 2048, 1536], P('batch', 'seq'), may hold values from -6 to 6
Outputs:
- output: bfloat16 [8, 2048, 1536], P('batch', 'seq')
- hidden_grad: bfloat16 [8, 2048, 1536], P('batch', 'seq')
- in_proj_grad: float32 [1536, 6448], P(('batch', 'seq'))
- out_proj_grad: float32 [3072, 1536], P(('batch', 'seq'))
- conv_weight_grad: float32 [4, 3328], P(None, ('batch', 'seq'))
- conv_bias_grad: float32 [3328], P(('batch', 'seq'))
- step_bias_grad: float32 [48], replicated
- decay_log_grad: float32 [48], replicated
- skip_weight_grad: float32 [48], replicated
- gated_gain_grad: float32 [3072], P(('batch', 'seq'))
- norm_gain_grad: float32 [1536], P(('batch', 'seq'))
The draws below stay inside these ranges and needn't reach their ends.
All inputs are finite; a program needn't handle non-finite values.
Results may differ from the reference program's by a relative error of at most 0.0096.
Values may be sent and summed in bfloat16 or wider, within the bound.
No kernel may reach another device: no remote copies, remote signals or barrier semaphores. Data moves between devices by JAX's collectives and lax.ppermute only.
A program may use at most 320 MiB of HBM per device.

```python
import math
import jax
import jax.numpy as jnp
from jax import lax

MODEL_DIM = 1536
HEAD_COUNT = 48
P_SIZE = 64
NS = 128
KCONV = 4
BLOCK = 256
TOKEN_LENGTH = 2048
DI = 3072
CONV_CH = 3328
PROJECT_COLUMNS = 6448
SEQUENCE_COUNT = 8


def spike_direction(key):
    return jnp.clip(jax.random.normal(jax.random.fold_in(key, 7), (MODEL_DIM,), jnp.float32), -4.0, 4.0)


def draw_hidden(key, part):
    noise_key = jax.random.fold_in(key, 11)
    baseline_jitter = jax.random.normal(noise_key, (SEQUENCE_COUNT, TOKEN_LENGTH, MODEL_DIM), jnp.float32)
    spike_locations = jax.random.randint(jax.random.fold_in(key, 17), (SEQUENCE_COUNT, 3), 0, TOKEN_LENGTH)
    spike_flags = jnp.any(jnp.arange(TOKEN_LENGTH)[None, :, None] == spike_locations[:, None, :], axis=-1)
    spike_row_list = spike_direction(key)[None, None, :] + 0.2 * jax.random.normal(jax.random.fold_in(key, 19), (SEQUENCE_COUNT, TOKEN_LENGTH, MODEL_DIM), jnp.float32)
    value_entries = jnp.where(spike_flags[:, :, None], spike_row_list, baseline_jitter)
    return jnp.clip(value_entries, -6.0, 6.0).astype(jnp.bfloat16)


def draw_in_proj(key, part):
    draw_key = jax.random.fold_in(key, 21)
    baseline_sample = jnp.clip(jax.random.normal(draw_key, (MODEL_DIM, PROJECT_COLUMNS), jnp.float32), -6.0, 6.0)
    baseline_sample = baseline_sample / math.sqrt(MODEL_DIM)
    spike_factor = jax.random.uniform(jax.random.fold_in(key, 23), (HEAD_COUNT,), jnp.float32, 8.0, 10.0)
    spike_portion = spike_direction(key)[:, None] * spike_factor[None, :] / MODEL_DIM
    step_column_slice = baseline_sample[:, PROJECT_COLUMNS - HEAD_COUNT:] + spike_portion
    return jnp.concatenate([baseline_sample[:, :PROJECT_COLUMNS - HEAD_COUNT], step_column_slice], axis=1).astype(jnp.bfloat16)


def draw_step_bias(key, part):
    slow_share = 0.5
    slow_heads = jax.random.bernoulli(jax.random.fold_in(key, 29), slow_share, (HEAD_COUNT,))
    slow_values = jax.random.uniform(jax.random.fold_in(key, 31), (HEAD_COUNT,), jnp.float32, -10.0, -8.0)
    fast_values = jax.random.uniform(jax.random.fold_in(key, 37), (HEAD_COUNT,), jnp.float32, -5.0, -3.0)
    return jnp.where(slow_heads, slow_values, fast_values).astype(jnp.float32)


def shard_levels(stream_key, extent, split, smallest, high):
    def one(dim, shards_of):
        heights = jax.random.uniform(jax.random.fold_in(jax.random.fold_in(stream_key, 6), dim), (shards_of,), jnp.float32, smallest / len(split), high / len(split))
        return jnp.repeat(jnp.exp(heights), extent[dim] // shards_of).reshape((-1,) + (1,) * (len(extent) - dim - 1))

    gain = one(*split[0])
    for cut in split[1:]:
        gain = gain * one(*cut)
    return gain


def noise(key, extent, width, bound, cuts=(), kind=jnp.bfloat16):
    array = jax.random.normal(key, extent, jnp.float32) * width
    if len(cuts) > 0:
        array = shard_levels(key, extent, cuts, -0.22, 0.18) * array
    return jnp.clip(array, min=-bound, max=bound).astype(kind)


def setup_inputs(seed: int = 0) -> dict:
    key_of = jax.random.split(jax.random.key(seed), 12)
    hidden = draw_hidden(jax.random.fold_in(key_of[11], 71), 0)
    in_proj = draw_in_proj(jax.random.fold_in(key_of[11], 71), 0)
    out_proj = noise(key_of[2], (DI, MODEL_DIM), DI ** -0.5, 0.109375, ((0, 32),))
    conv_weight = noise(key_of[3], (KCONV, CONV_CH), KCONV ** -0.5, 3.0, ((1, 32),))
    conv_bias = noise(key_of[4], (CONV_CH,), 0.3, 1.5, ((0, 32),))
    step_bias = draw_step_bias(jax.random.fold_in(key_of[11], 71), 0)
    decay_log = jnp.clip(jax.random.uniform(key_of[6], (HEAD_COUNT,), jnp.float32, -1.2, 0.7), -1.2, 0.7)
    skip_weight = jnp.clip(jax.random.uniform(key_of[7], (HEAD_COUNT,), jnp.float32, 0.2, 1.5), 0.2, 1.5)
    gated_gain = jnp.clip(1.0 + 0.1 * jax.random.normal(key_of[8], (DI,), jnp.float32), 0.5, 1.5).astype(jnp.bfloat16)
    norm_gain = jnp.clip(1.0 + 0.1 * jax.random.normal(key_of[9], (MODEL_DIM,), jnp.float32), 0.5, 1.5).astype(jnp.bfloat16)
    cotangent = noise(key_of[10], (SEQUENCE_COUNT, TOKEN_LENGTH, MODEL_DIM), 1.0, 6.0, ((0, 8), (1, 4)))
    return dict(hidden=hidden, in_proj=in_proj, out_proj=out_proj, conv_weight=conv_weight, conv_bias=conv_bias, step_bias=step_bias, decay_log=decay_log, skip_weight=skip_weight, gated_gain=gated_gain, norm_gain=norm_gain, cotangent=cotangent)


EPSILON = 1e-05
HIGHEST = lax.Precision.HIGHEST

def prenorm(stream, norm_scale):
    return stream * lax.rsqrt(lax.optimization_barrier(jnp.mean(stream * stream, axis=-1, keepdims=True)) + EPSILON) * norm_scale

def scan_states(head_inputs, write_map, read_map, step_size, log_decay):
    row_count = head_inputs.shape[0]
    block_count = row_count // BLOCK
    scaled_x = (head_inputs * step_size[:, :, None]).reshape(block_count, BLOCK, HEAD_COUNT, P_SIZE)
    write_blocks = write_map.reshape(block_count, BLOCK, NS)
    read_blocks = read_map.reshape(block_count, BLOCK, NS)
    decay_blocks = log_decay.reshape(block_count, BLOCK, HEAD_COUNT)
    causal = jnp.arange(BLOCK)[:, None] >= jnp.arange(BLOCK)[None, :]

    def one_block(running, pieces):
        x_part, write_part, read_part, decay_part = pieces
        within = jnp.cumsum(decay_part, axis=0)
        across = within.T
        weights = jnp.exp(jnp.where(causal[None], across[:, :, None] - across[:, None, :], -jnp.inf))
        scores = jnp.dot(read_part, write_part.T, precision=HIGHEST)
        y_inside = jnp.einsum('hts,shp->thp', weights * scores[None], x_part, precision=HIGHEST)
        y_carried = jnp.exp(within)[:, :, None] * jnp.einsum('tn,hpn->thp', read_part, running, precision=HIGHEST)
        to_end = jnp.exp(within[-1:] - within)
        updated = jnp.exp(within[-1])[:, None, None] * running + jnp.einsum('sh,shp,sn->hpn', to_end, x_part, write_part, precision=HIGHEST)
        return (updated, y_inside + y_carried)
    initial = jnp.zeros((HEAD_COUNT, P_SIZE, NS), jnp.float32)
    _, outputs = lax.scan(one_block, initial, (scaled_x, write_blocks, read_blocks, decay_blocks))
    return outputs.reshape(row_count, HEAD_COUNT, P_SIZE)

def mixer(projected, conv_kernel, conv_offset, step_bias, decay_log, skip_weight, gated_scale):
    row_count = projected.shape[0]
    gate_part = projected[:, :DI]
    conv_part = projected[:, DI:DI + CONV_CH]
    raw_step = projected[:, DI + CONV_CH:]
    extended = jnp.concatenate([jnp.zeros((KCONV - 1, CONV_CH), jnp.float32), conv_part], axis=0)
    convolved = conv_offset + conv_kernel[0] * extended[0:row_count]
    for offset in range(1, KCONV):
        convolved = convolved + conv_kernel[offset] * extended[offset:offset + row_count]
    active = jax.nn.silu(convolved)
    head_inputs = active[:, :DI].reshape(row_count, HEAD_COUNT, P_SIZE)
    write_map = active[:, DI:DI + NS]
    read_map = active[:, DI + NS:]
    step_size = jax.nn.softplus(raw_step + step_bias)
    log_decay = -jnp.exp(decay_log) * step_size
    mixed_y = scan_states(head_inputs, write_map, read_map, step_size, log_decay) + skip_weight[None, :, None] * head_inputs
    gated_v = mixed_y.reshape(row_count, DI) * jax.nn.silu(gate_part)
    return gated_v * lax.rsqrt(lax.optimization_barrier(jnp.mean(gated_v * gated_v, axis=-1, keepdims=True)) + EPSILON) * gated_scale

def reference(hidden, in_proj, out_proj, conv_weight, conv_bias, step_bias, decay_log, skip_weight, gated_gain, norm_gain, cotangent):
    conv_kernel = conv_weight.astype(jnp.float32)
    conv_offset = conv_bias.astype(jnp.float32)
    gated_scale = gated_gain.astype(jnp.float32)
    norm_scale = norm_gain.astype(jnp.float32)

    def one_sequence(totals, pieces):
        stream_low, upstream = pieces
        stream = stream_low.astype(jnp.float32)
        normed, norm_pull = jax.vjp(prenorm, stream, norm_scale)
        normed_low = normed.astype(jnp.bfloat16)
        projected = jnp.dot(normed_low, in_proj, preferred_element_type=jnp.float32)
        gated_out, mixer_pull = jax.vjp(mixer, projected, conv_kernel, conv_offset, step_bias, decay_log, skip_weight, gated_scale)
        gated_low = gated_out.astype(jnp.bfloat16)
        output = (stream + jnp.dot(gated_low, out_proj, preferred_element_type=jnp.float32)).astype(jnp.bfloat16)
        grad_gated = jnp.dot(upstream, out_proj.T, preferred_element_type=jnp.float32)
        grad_out_w = jnp.dot(gated_low.T, upstream, preferred_element_type=jnp.float32)
        grad_proj, grad_kernel, grad_offset, grad_bias, grad_rate, grad_skip, grad_gated_scale = mixer_pull(grad_gated)
        grad_proj_low = grad_proj.astype(jnp.bfloat16)
        grad_in_w = jnp.dot(normed_low.T, grad_proj_low, preferred_element_type=jnp.float32)
        grad_normed = jnp.dot(grad_proj_low, in_proj.T, preferred_element_type=jnp.float32)
        grad_stream, grad_norm_scale = norm_pull(grad_normed)
        hidden_grad = (upstream.astype(jnp.float32) + grad_stream).astype(jnp.bfloat16)
        partials = (grad_in_w, grad_out_w, grad_kernel, grad_offset, grad_bias, grad_rate, grad_skip, grad_gated_scale, grad_norm_scale)
        return (jax.tree.map(jnp.add, totals, partials), (output, hidden_grad))
    initial = (jnp.zeros((MODEL_DIM, PROJECT_COLUMNS), jnp.float32), jnp.zeros((DI, MODEL_DIM), jnp.float32), jnp.zeros((KCONV, CONV_CH), jnp.float32), jnp.zeros((CONV_CH,), jnp.float32), jnp.zeros((HEAD_COUNT,), jnp.float32), jnp.zeros((HEAD_COUNT,), jnp.float32), jnp.zeros((HEAD_COUNT,), jnp.float32), jnp.zeros((DI,), jnp.float32), jnp.zeros((MODEL_DIM,), jnp.float32))
    totals, results = lax.scan(one_sequence, initial, (hidden, cotangent))
    return (results[0], results[1], totals[0], totals[1], totals[2], totals[3], totals[4], totals[5], totals[6], totals[7], totals[8])
```

```python
import functools

import jax
import jax.numpy as jnp
from jax import lax
from jax.experimental import pallas as pl
from jax.experimental.pallas import tpu as pltpu
from jax.sharding import PartitionSpec as P

EPSILON = 1e-05
HIGHEST = lax.Precision.HIGHEST
AXES = ("batch", "seq")
F32 = jnp.float32
BF16 = jnp.bfloat16
L = 128
LANES = 128

PG, PS, PM, PO, PC = 3, 3, 3, 1, 1
ENTER = F32 if PS > 1 else BF16
VMEM_LIMIT = 60 * 1024 * 1024


def dot(a, b, ca=1, cb=0):
    return lax.dot_general(a, b, (((ca,), (cb,)), ((), ())), preferred_element_type=F32)


def halves(a):
    high = a.astype(BF16)
    return high, (a - high.astype(F32)).astype(BF16)


def mm(a, b, ca=1, cb=0, parts=1):
    if parts == 1:
        return dot(a.astype(BF16), b.astype(BF16), ca, cb)
    a_high, a_low = halves(a)
    b_high, b_low = halves(b)
    return dot(a_high, b_high, ca, cb) + (dot(a_low, b_high, ca, cb) + dot(a_high, b_low, ca, cb))


def dot_exact(a, b):
    return lax.dot_general(
        a, b, (((1,), (0,)), ((), ())), precision=HIGHEST, preferred_element_type=F32
    )


def dot_split(a, b):
    high = a.astype(BF16)
    low = (a - high.astype(F32)).astype(BF16)
    return dot(high, b) + dot(low, b)


def rounded(a, parts):
    return a if parts > 1 else a.astype(BF16).astype(F32)


def iota(shape, dim):
    return lax.broadcasted_iota(jnp.int32, shape, dim)


def sigmoid(v):
    return 1.0 / (1.0 + jnp.exp(-v))


def softplus(v):
    return jnp.maximum(v, 0.0) + jnp.log1p(jnp.exp(-jnp.abs(v)))


def column(value, lane):
    return jnp.broadcast_to(value[:, lane : lane + 1], (value.shape[0], LANES))


def pair_lanes(first, second):
    return jnp.where(iota(first.shape, 1) < LANES // 2, first, second)


def earlier(value, tail, steps):
    turned = pltpu.roll(value, steps, 0)
    head = jnp.where(iota(tail.shape, 0) < steps, pltpu.roll(tail, steps, 0), turned[:8])
    return jnp.concatenate([head, turned[8:]], axis=0)


def later(value, following, steps):
    rows = value.shape[0]
    turned = pltpu.roll(value, rows - steps, 0)
    end = jnp.where(
        iota(following.shape, 0) >= 8 - steps,
        pltpu.roll(following, 8 - steps, 0),
        turned[rows - 8 :],
    )
    return jnp.concatenate([turned[: rows - 8], end], axis=0)


def forward_body(
    width, state, taps, per_seq, p_ref, conv_ref, head_ref, lane_ref,
    v_ref, y_ref, u_ref, square_ref, enter_ref, tail, run,
):
    channels = width + 2 * state
    pairs = width // LANES

    @pl.when(pl.program_id(0) % per_seq == 0)
    def _():
        tail[...] = jnp.zeros_like(tail)
        run[...] = jnp.zeros_like(run)

    conv_in = p_ref[:, width : width + channels]
    before = tail[...]
    convolved = conv_ref[taps : taps + 1] + conv_ref[taps - 1 : taps] * conv_in
    for steps in range(1, taps):
        convolved = convolved + conv_ref[taps - 1 - steps : taps - steps] * earlier(
            conv_in, before, steps
        )
    tail[...] = conv_in[L - 8 :]
    v_ref[...] = convolved
    active = convolved * sigmoid(convolved)
    x = active[:, :width]
    write = active[:, width : width + state]
    read = active[:, width + state :]
    step = softplus(p_ref[:, width + channels :] + head_ref[0:1])
    causal = iota((L, L), 0) >= iota((L, L), 1)
    cum = dot_exact(causal.astype(F32), step * head_ref[1:2])
    cum_rows = cum.T
    scores = mm(read, write, 1, 1, PG)
    running = run[...]
    enter_ref[...] = running.astype(enter_ref.dtype)
    carried = mm(read, running, 1, 0, PS)
    first_half = iota((L, LANES), 1) < LANES // 2
    to_state, decays, y_parts = [], [], []
    for q in range(pairs):
        weights, columns = [], []
        for h in (2 * q, 2 * q + 1):
            col = column(cum, h)
            columns.append(col)
            gap = jnp.where(causal, col - cum_rows[h : h + 1], -jnp.inf)
            weights.append(jnp.exp(gap) * scores)
        cum_pair = pair_lanes(*columns)
        step_pair = pair_lanes(column(step, 2 * q), column(step, 2 * q + 1))
        span = slice(q * LANES, (q + 1) * LANES)
        scaled = x[:, span] * step_pair
        inside = mm(
            jnp.concatenate(weights, axis=1),
            jnp.concatenate(
                [jnp.where(first_half, scaled, 0.0), jnp.where(first_half, 0.0, scaled)], axis=0
            ),
            1, 0, PM,
        )
        last = cum_pair[L - 1 :]
        to_state.append(scaled * jnp.exp(last - cum_pair))
        decays.append(jnp.exp(last))
        y_parts.append(inside + jnp.exp(cum_pair) * carried[:, span])
    y = jnp.concatenate(y_parts, axis=1)
    y_ref[...] = y
    run[...] = jnp.concatenate(decays, axis=1) * running + mm(
        write, jnp.concatenate(to_state, axis=1), 0, 0, PS
    )
    gate = p_ref[:, :width]
    mixed = y + lane_ref[0:1] * x
    gated = mixed * (gate * sigmoid(gate))
    u_ref[...] = (gated * lane_ref[1:2]).astype(BF16)
    squares = gated * gated
    total = squares[:, :LANES]
    for q in range(1, pairs):
        total = total + squares[:, q * LANES : (q + 1) * LANES]
    square_ref[...] = total


def backward_body(
    width, state, taps, per_seq, p_ref, v_ref, y_ref, enter_ref, grad_ref, stat_ref,
    conv_ref, head_ref, lane_ref, expand_ref,
    gp_ref, conv_acc, lane_acc, head_acc, ahead, run, leaving,
):
    channels = width + 2 * state
    pairs = width // LANES

    @pl.when(pl.program_id(0) == 0)
    def _():
        conv_acc[...] = jnp.zeros_like(conv_acc)
        lane_acc[...] = jnp.zeros_like(lane_acc)
        head_acc[...] = jnp.zeros_like(head_acc)

    @pl.when(pl.program_id(0) % per_seq == 0)
    def _():
        ahead[...] = jnp.zeros_like(ahead)
        run[...] = jnp.zeros_like(run)
        leaving[...] = jnp.zeros_like(leaving)

    convolved = v_ref[...]
    bend = sigmoid(convolved)
    active = convolved * bend
    slope = bend * (1.0 + convolved * (1.0 - bend))
    x = active[:, :width]
    write = active[:, width : width + state]
    read = active[:, width + state :]
    raw = p_ref[:, width + channels :] + head_ref[0:1]
    rate = head_ref[1:2]
    step = softplus(raw)
    log_decay = step * rate
    upper = iota((L, L), 0) <= iota((L, L), 1)
    lower = iota((L, L), 0) >= iota((L, L), 1)
    cum = dot_exact(lower.astype(F32), log_decay)
    cum_rows = cum.T

    gate = p_ref[:, :width]
    y = y_ref[...]
    grad = grad_ref[...]
    gate_bend = sigmoid(gate)
    gate_silu = gate * gate_bend
    mixed = y + lane_ref[0:1] * x
    gated = mixed * gate_silu
    inverse = jnp.broadcast_to(stat_ref[:, 0:1], (L, width))
    pull = jnp.broadcast_to(stat_ref[:, 1:2], (L, width))
    scaled_grad = inverse * grad
    grad_gated = scaled_grad * lane_ref[1:2] - gated * pull
    gp_ref[:, :width] = (
        grad_gated * mixed * (gate_bend * (1.0 + gate * (1.0 - gate_bend)))
    ).astype(BF16)
    grad_y = grad_gated * gate_silu
    lane_acc[0:1] += jnp.sum(scaled_grad * gated, axis=0, keepdims=True)
    lane_acc[1:2] += jnp.sum(grad_y * x, axis=0, keepdims=True)
    grad_low = rounded(grad_y, PM)

    scores = mm(write, read, 1, 1, PG)
    grad_state = run[...]
    from_state = mm(write, grad_state, 1, 0, PS)
    entering = enter_ref[...]
    first_half = iota((L, LANES), 1) < LANES // 2
    grad_scores = jnp.zeros((L, L), F32)
    to_state, grad_carried, decays, grad_scaled, lows, steps = [], [], [], [], [], []
    for q in range(pairs):
        span = slice(q * LANES, (q + 1) * LANES)
        step_pair = pair_lanes(column(step, 2 * q), column(step, 2 * q + 1))
        scaled = x[:, span] * step_pair
        low = rounded(scaled, PM)
        dy = grad_low[:, span]
        outer = mm(
            jnp.concatenate(
                [jnp.where(first_half, low, 0.0), jnp.where(first_half, 0.0, low)], axis=0
            ),
            dy,
            1,
            1,
            PO,
        )
        weights, columns = [], []
        for k in range(2):
            h = 2 * q + k
            col = column(cum, h)
            columns.append(col)
            decay = jnp.exp(jnp.where(upper, cum_rows[h : h + 1] - col, -jnp.inf))
            weights.append(decay * scores)
            grad_scores = grad_scores + decay * outer[k * L : (k + 1) * L]
        inside = mm(
            jnp.concatenate(weights, axis=1),
            jnp.concatenate(
                [jnp.where(first_half, dy, 0.0), jnp.where(first_half, 0.0, dy)], axis=0
            ),
            1,
            0,
            PM,
        )
        cum_pair = pair_lanes(*columns)
        last = cum_pair[L - 1 :]
        to_end = jnp.exp(last - cum_pair)
        to_state.append(scaled * to_end)
        grad_carried.append(grad_y[:, span] * jnp.exp(cum_pair))
        decays.append(jnp.exp(last))
        grad_scaled.append(inside + to_end * from_state[:, span])
        lows.append(low)
        steps.append(step_pair)
    grad_scaled = jnp.concatenate(grad_scaled, axis=1)
    to_state = jnp.concatenate(to_state, axis=1)
    grad_carried = jnp.concatenate(grad_carried, axis=1)
    lows = jnp.concatenate(lows, axis=1)
    steps = jnp.concatenate(steps, axis=1)
    grad_write = mm(grad_scores, read, 1, 0, PO) + mm(to_state, grad_state, 1, 1, PC)
    grad_read = mm(grad_scores, write, 0, 0, PO) + mm(grad_carried, entering, 1, 1, PC)
    across = jnp.sum(leaving[...].astype(F32) * grad_state, axis=0, keepdims=True)
    run[...] = jnp.concatenate(decays, axis=1) * grad_state + mm(read, grad_carried, 0, 0, PS)
    leaving[...] = entering

    rows = jnp.concatenate(
        [
            y * grad_low - lows * grad_scaled,
            x * grad_scaled,
            jnp.broadcast_to(across, (8, width)),
        ],
        axis=0,
    )
    by_head = dot_split(rows, expand_ref[...])
    grad_decay = dot_split_left(upper.astype(BF16), by_head[:L]) + by_head[2 * L : 2 * L + 1]
    grad_step = by_head[L : 2 * L] + rate * grad_decay
    grad_raw = grad_step * sigmoid(raw)
    head_acc[0:1] += jnp.sum(grad_raw, axis=0, keepdims=True)
    head_acc[1:2] += jnp.sum(grad_decay * log_decay, axis=0, keepdims=True)
    gp_ref[:, width + channels :] = grad_raw.astype(BF16)

    grad_x = grad_scaled * steps + lane_ref[0:1] * grad_y
    grad_conv = jnp.concatenate([grad_x, grad_write, grad_read], axis=1) * slope
    following = ahead[...]
    conv_in = p_ref[:, width : width + channels]
    total = conv_ref[taps - 1 : taps] * grad_conv
    conv_acc[taps - 1 : taps] += jnp.sum(grad_conv * conv_in, axis=0, keepdims=True)
    conv_acc[taps : taps + 1] += jnp.sum(grad_conv, axis=0, keepdims=True)
    for steps_on in range(1, taps):
        moved = later(grad_conv, following, steps_on)
        row = taps - 1 - steps_on
        total = total + conv_ref[row : row + 1] * moved
        conv_acc[row : row + 1] += jnp.sum(moved * conv_in, axis=0, keepdims=True)
    ahead[...] = grad_conv[:8]
    gp_ref[:, width : width + channels] = total.astype(BF16)


def dot_split_left(a, b):
    high = b.astype(BF16)
    low = (b - high.astype(F32)).astype(BF16)
    return dot(a, high) + dot(a, low)


def forward_scan(projected, conv_rows, head_rows, lane_rows, width, state, taps, per_seq):
    tokens, columns = projected.shape
    blocks = tokens // L
    channels = width + 2 * state
    whole = lambda i: (0, 0)
    mine = lambda i: (i, 0)
    return pl.pallas_call(
        functools.partial(forward_body, width, state, taps, per_seq),
        grid=(blocks,),
        in_specs=[
            pl.BlockSpec((L, columns), mine),
            pl.BlockSpec(conv_rows.shape, whole),
            pl.BlockSpec(head_rows.shape, whole),
            pl.BlockSpec(lane_rows.shape, whole),
        ],
        out_specs=[
            pl.BlockSpec((L, channels), mine),
            pl.BlockSpec((L, width), mine),
            pl.BlockSpec((L, width), mine),
            pl.BlockSpec((L, LANES), mine),
            pl.BlockSpec((state, width), mine),
        ],
        out_shape=[
            jax.ShapeDtypeStruct((tokens, channels), F32),
            jax.ShapeDtypeStruct((tokens, width), F32),
            jax.ShapeDtypeStruct((tokens, width), BF16),
            jax.ShapeDtypeStruct((tokens, LANES), F32),
            jax.ShapeDtypeStruct((blocks * state, width), ENTER),
        ],
        scratch_shapes=[pltpu.VMEM((8, channels), F32), pltpu.VMEM((state, width), F32)],
        compiler_params=pltpu.CompilerParams(
            dimension_semantics=("arbitrary",), vmem_limit_bytes=VMEM_LIMIT
        ),
        cost_estimate=pl.CostEstimate(
            flops=tokens * width * 1024, bytes_accessed=tokens * columns * 10, transcendentals=0
        ),
        name="forward_scan",
    )(projected, conv_rows, head_rows, lane_rows)


def backward_scan(
    projected, convolved, y, entering, grad, stats, conv_rows, head_rows, lane_rows, expand,
    width, state, taps, per_seq,
):
    tokens, columns = projected.shape
    blocks = tokens // L
    channels = width + 2 * state
    whole = lambda i: (0, 0)
    mine = lambda i: (blocks - 1 - i, 0)
    return pl.pallas_call(
        functools.partial(backward_body, width, state, taps, per_seq),
        grid=(blocks,),
        in_specs=[
            pl.BlockSpec((L, columns), mine),
            pl.BlockSpec((L, channels), mine),
            pl.BlockSpec((L, width), mine),
            pl.BlockSpec((state, width), mine),
            pl.BlockSpec((L, width), mine),
            pl.BlockSpec((L, stats.shape[1]), mine),
            pl.BlockSpec(conv_rows.shape, whole),
            pl.BlockSpec(head_rows.shape, whole),
            pl.BlockSpec(lane_rows.shape, whole),
            pl.BlockSpec(expand.shape, whole),
        ],
        out_specs=[
            pl.BlockSpec((L, columns), mine),
            pl.BlockSpec(conv_rows.shape, whole),
            pl.BlockSpec(lane_rows.shape, whole),
            pl.BlockSpec(head_rows.shape, whole),
        ],
        out_shape=[
            jax.ShapeDtypeStruct((tokens, columns), BF16),
            jax.ShapeDtypeStruct(conv_rows.shape, F32),
            jax.ShapeDtypeStruct(lane_rows.shape, F32),
            jax.ShapeDtypeStruct(head_rows.shape, F32),
        ],
        scratch_shapes=[
            pltpu.VMEM((8, channels), F32),
            pltpu.VMEM((state, width), F32),
            pltpu.VMEM((state, width), ENTER),
        ],
        compiler_params=pltpu.CompilerParams(
            dimension_semantics=("arbitrary",), vmem_limit_bytes=VMEM_LIMIT
        ),
        cost_estimate=pl.CostEstimate(
            flops=tokens * width * 3072, bytes_accessed=tokens * columns * 14, transcendentals=0
        ),
        name="backward_scan",
    )(projected, convolved, y, entering, grad, stats, conv_rows, head_rows, lane_rows, expand)


def rows_of(vectors, lanes):
    made = [jnp.pad(v.astype(F32), ((0, 0), (0, lanes - v.shape[1]))) for v in vectors]
    stacked = jnp.concatenate(made, axis=0)
    return jnp.pad(stacked, ((0, 8 - stacked.shape[0]), (0, 0)))


def send(value, sizes, move):
    nb, ns = sizes
    pairs = []
    for b in range(nb):
        for s in range(ns):
            goal = move(b, s)
            if goal is not None:
                pairs.append((b * ns + s, goal[0] * ns + goal[1]))
    return lax.ppermute(value, AXES, pairs)


def swap_core(value, sizes):
    return send(value, sizes, lambda b, s: (b, s ^ 1))


def turn_row(value, sizes, k):
    return send(value, sizes, lambda b, s: (b, (s + 2 * k) % sizes[1]))


def gather_pieces(piece, sizes):
    ns = sizes[1]
    me = lax.axis_index("seq")
    place = lambda total, part, at: lax.dynamic_update_index_in_dim(total, part, at, 0)
    total = jnp.zeros((ns,) + piece.shape, piece.dtype)
    got = [piece] + [turn_row(piece, sizes, k) for k in range(1, ns // 2)]
    for k, part in enumerate(got):
        at = (me + ns - 2 * k) % ns
        total = place(total, part, at)
        total = place(total, swap_core(part, sizes), at ^ 1)
    return total


def scatter_pieces(value, sizes):
    ns = sizes[1]
    me = lax.axis_index("seq")
    chip, core = me // 2, me % 2
    split = value.reshape((ns // 2, 2) + value.shape[1:])
    give = lax.dynamic_index_in_dim(split, 1 - core, 1, False).astype(BF16)
    keep = lax.dynamic_index_in_dim(split, core, 1, False)
    both = keep + swap_core(give, sizes).astype(F32)
    total = lax.dynamic_index_in_dim(both, chip, 0, False)
    for k in range(1, ns // 2):
        part = lax.dynamic_index_in_dim(both, (chip + k) % (ns // 2), 0, False)
        total = total + turn_row(part.astype(BF16), sizes, k).astype(F32)
    return total


def add_over(value, sizes, axis):
    k = 1
    while k < sizes[axis]:
        step = k
        if axis == 0:
            value = value + send(value, sizes, lambda b, s: (b ^ step, s))
        else:
            value = value + send(value, sizes, lambda b, s: (b, s ^ step))
        k *= 2
    return value


def collect_over_seq(value, sizes):
    ns = sizes[1]
    me = lax.axis_index("seq")
    total = lax.dynamic_update_index_in_dim(
        jnp.zeros((ns,) + value.shape, value.dtype), value, me, 0
    )
    return add_over(total, sizes, 1)


def per_device(
    sizes, hidden, in_proj, out_proj, conv_weight, conv_bias, step_bias, decay_log,
    skip_weight, gated_gain, norm_gain, cotangent,
):
    nb, ns = sizes
    devices = nb * ns
    me_b, me_s = lax.axis_index("batch"), lax.axis_index("seq")
    seq_count, piece, model = hidden.shape
    taps, conv_part = conv_weight.shape
    conv_channels = conv_part * devices
    inner = out_proj.shape[0] * devices
    heads = step_bias.shape[0]
    state = (conv_channels - inner) // 2
    in_rows = in_proj.shape[0]
    own_heads = heads // ns
    width = inner // ns
    head_size = inner // heads
    channels = width + 2 * state
    columns = width + channels + LANES
    tokens = seq_count * piece * ns
    per_seq = piece * ns // L

    dt_at = inner + conv_channels
    payload = jnp.stack(
        [
            jnp.concatenate(
                [
                    in_proj[:, s * width : (s + 1) * width],
                    in_proj[:, inner + s * width : inner + (s + 1) * width],
                    in_proj[:, 2 * inner : dt_at],
                    jnp.pad(
                        in_proj[:, dt_at + s * own_heads : dt_at + (s + 1) * own_heads],
                        ((0, 0), (0, LANES - own_heads)),
                    ),
                ],
                axis=1,
            )
            for s in range(ns)
        ]
    )
    mine = lax.all_to_all(payload, "seq", 0, 0, tiled=False).reshape(ns * in_rows, columns)
    weight_in = lax.all_gather(mine, "batch", axis=0, tiled=True)
    out_rows = lax.ppermute(
        out_proj, AXES, [(j, (j % nb) * ns + j // nb) for j in range(devices)]
    )
    weight_out = lax.all_gather(out_rows, "batch", axis=0, tiled=True)

    small = jnp.concatenate(
        [conv_weight.reshape(-1), conv_bias.reshape(-1), gated_gain, norm_gain]
    ).reshape(1, -1)
    small = lax.all_gather(small, "seq", axis=0, tiled=True)
    small = lax.all_gather(small, "batch", axis=0, tiled=True).astype(F32)
    conv_all = jnp.moveaxis(
        small[:, : taps * conv_part].reshape(devices, taps, conv_part), 0, 1
    ).reshape(taps, conv_channels)
    at = taps * conv_part
    bias_all = small[:, at : at + conv_part].reshape(1, conv_channels)
    at += conv_part
    gain_all = small[:, at : at + gated_gain.shape[0]].reshape(1, inner)
    at += gated_gain.shape[0]
    norm_all = small[:, at:].reshape(1, model)
    conv_all = jnp.concatenate([conv_all, bias_all], axis=0)
    conv_rows = rows_of(
        [
            jnp.concatenate(
                [
                    lax.dynamic_slice_in_dim(conv_all, me_s * width, width, 1),
                    conv_all[:, inner:],
                ],
                axis=1,
            )
        ],
        channels,
    )
    own = lambda v: lax.dynamic_slice_in_dim(v, me_s * own_heads, own_heads, 0)
    head_rows = rows_of([own(step_bias)[None], -jnp.exp(own(decay_log))[None]], LANES)
    lane_rows = rows_of(
        [
            jnp.repeat(own(skip_weight), head_size)[None],
            lax.dynamic_slice_in_dim(gain_all, me_s * width, width, 1),
        ],
        width,
    )
    expand = (
        jnp.arange(width)[:, None] // head_size == jnp.arange(LANES)[None, :]
    ).astype(BF16)

    stream = hidden.reshape(-1, model).astype(F32)
    spread = lax.rsqrt(jnp.mean(stream * stream, axis=-1, keepdims=True) + EPSILON)
    normed = (stream * spread * norm_all).astype(BF16)

    def in_order(pieces):
        value = pieces.reshape((ns, seq_count, piece, model))
        return jnp.swapaxes(value, 0, 1).reshape(tokens, model)

    def in_pieces(value):
        value = value.reshape((seq_count, ns, piece, model))
        return jnp.swapaxes(value, 0, 1).reshape(ns, seq_count * piece, model)

    normed_all = in_order(gather_pieces(normed, sizes))
    upstream = in_order(gather_pieces(cotangent.reshape(-1, model), sizes))

    projected = jnp.dot(normed_all, weight_in, preferred_element_type=F32)
    convolved, y, ungained, squares, entering = forward_scan(
        projected, conv_rows, head_rows, lane_rows, width, state, taps, per_seq
    )
    grad_gated = jnp.einsum("td,kd->tk", upstream, weight_out, preferred_element_type=F32)
    sums = jnp.stack(
        [
            jnp.sum(squares, axis=1),
            jnp.sum(grad_gated * ungained.astype(F32), axis=1),
        ]
    )
    sums = add_over(sums, sizes, 1)
    inverse = lax.rsqrt(sums[0] / inner + EPSILON)
    pull = inverse * inverse * inverse * sums[1] / inner
    stats = jnp.stack([inverse, pull], axis=1)
    out_partial = jnp.dot(ungained, weight_out, preferred_element_type=F32)
    out_sum = scatter_pieces(in_pieces(out_partial), sizes)
    own_inverse = lax.dynamic_index_in_dim(
        jnp.swapaxes(inverse.reshape(seq_count, ns, piece), 0, 1), me_s, 0, False
    ).reshape(-1, 1)
    result = (stream + own_inverse * out_sum).astype(BF16)
    gated_low = (ungained.astype(F32) * inverse[:, None]).astype(BF16)
    grad_out_w = jnp.einsum("tk,td->kd", gated_low, upstream, preferred_element_type=F32)

    grad_proj, conv_acc, lane_acc, head_acc = backward_scan(
        projected, convolved, y, entering, grad_gated, stats, conv_rows, head_rows, lane_rows,
        expand, width, state, taps, per_seq,
    )
    grad_in_w = jnp.einsum("td,tk->dk", normed_all, grad_proj, preferred_element_type=F32)
    grad_normed = jnp.einsum("tk,dk->td", grad_proj, weight_in, preferred_element_type=F32)
    grad_normed = scatter_pieces(in_pieces(grad_normed), sizes)
    scaled = grad_normed * norm_all
    unit = stream * spread
    grad_stream = spread * (scaled - unit * jnp.mean(scaled * unit, axis=-1, keepdims=True))
    hidden_grad = (cotangent.reshape(-1, model).astype(F32) + grad_stream).astype(BF16)

    out_part = lax.psum_scatter(
        grad_out_w.astype(BF16), "batch", scatter_dimension=0, tiled=True
    )
    out_proj_grad = lax.ppermute(
        out_part, AXES, [((j % nb) * ns + j // nb, j) for j in range(devices)]
    ).astype(F32)
    in_part = lax.psum_scatter(grad_in_w.astype(BF16), "batch", scatter_dimension=0, tiled=True)
    by_source = lax.all_to_all(
        in_part.reshape(ns, in_rows, columns), "seq", 0, 0, tiled=False
    ).astype(F32)
    across = lambda lo, hi: jnp.concatenate([by_source[s, :, lo:hi] for s in range(ns)], axis=1)
    in_proj_grad = jnp.concatenate(
        [
            across(0, width),
            across(width, 2 * width),
            jnp.sum(by_source[:, :, 2 * width : width + channels], axis=0),
            across(width + channels, width + channels + own_heads),
        ],
        axis=1,
    )
    norm_gain_grad = jnp.sum(in_proj.astype(F32) * in_proj_grad, axis=1) / norm_gain.astype(F32)

    by_head = jnp.sum(lane_acc[1].reshape(own_heads, head_size), axis=1)
    packed = jnp.concatenate(
        [
            conv_acc[: taps + 1].reshape(-1),
            lane_acc[0],
            by_head,
            head_acc[0, :own_heads],
            head_acc[1, :own_heads],
        ]
    )
    packed = jnp.pad(packed, (0, -packed.shape[0] % (8 * LANES))).reshape(-1, LANES)
    packed = collect_over_seq(add_over(packed, sizes, 0), sizes).reshape(ns, -1)
    rows = (taps + 1) * channels
    conv_grads = packed[:, :rows].reshape(ns, taps + 1, channels)
    conv_grads = jnp.concatenate(
        [
            jnp.moveaxis(conv_grads[:, :, :width], 0, 1).reshape(taps + 1, inner),
            jnp.sum(conv_grads[:, :, width:], axis=0),
        ],
        axis=1,
    )
    me = me_b * ns + me_s
    conv_grads = lax.dynamic_slice_in_dim(conv_grads, me * conv_part, conv_part, 1)
    gain_grad = lax.dynamic_slice_in_dim(
        packed[:, rows : rows + width].reshape(-1), me * gated_gain.shape[0], gated_gain.shape[0], 0
    )
    at = rows + width
    skip_grad, bias_grad, rate_grad = (
        packed[:, at + k * own_heads : at + (k + 1) * own_heads].reshape(-1) for k in range(3)
    )
    return (
        result.reshape(hidden.shape),
        hidden_grad.reshape(hidden.shape),
        in_proj_grad,
        out_proj_grad,
        conv_grads[:taps],
        conv_grads[taps],
        bias_grad,
        rate_grad,
        skip_grad,
        gain_grad,
        norm_gain_grad,
    )


def solution(mesh):
    both = P(AXES)
    in_specs = (
        P("batch", "seq", None),
        P(AXES, None),
        P(AXES, None),
        P(None, AXES),
        both,
        P(),
        P(),
        P(),
        both,
        both,
        P("batch", "seq", None),
    )
    out_specs = (
        P("batch", "seq", None),
        P("batch", "seq", None),
        P(AXES, None),
        P(AXES, None),
        P(None, AXES),
        both,
        P(),
        P(),
        P(),
        both,
        both,
    )
    sizes = (mesh.shape["batch"], mesh.shape["seq"])
    return jax.shard_map(
        functools.partial(per_device, sizes),
        mesh=mesh,
        in_specs=in_specs,
        out_specs=out_specs,
        check_vma=False,
    )
```

```python
import functools

import jax
import jax.numpy as jnp
from jax import lax
from jax.experimental import pallas as pl
from jax.experimental.pallas import tpu as pltpu
from jax.sharding import PartitionSpec as P


EPSILON = 1e-05
HIGHEST = lax.Precision.HIGHEST
AXES = ("batch", "seq")
F32 = jnp.float32
BF16 = jnp.bfloat16
L = 128
LANES = 128

PG, PS, PM, PO, PC = 3, 3, 3, 1, 1
ENTER = F32 if PS > 1 else BF16
VMEM_LIMIT = 60 * 1024 * 1024


def dot(a, b, ca=1, cb=0):
    return lax.dot_general(a, b, (((ca,), (cb,)), ((), ())), preferred_element_type=F32)


def halves(a):
    high = a.astype(BF16)
    return high, (a - high.astype(F32)).astype(BF16)


def mm(a, b, ca=1, cb=0, parts=1):
    if parts == 1:
        return dot(a.astype(BF16), b.astype(BF16), ca, cb)
    a_high, a_low = halves(a)
    b_high, b_low = halves(b)
    return dot(a_high, b_high, ca, cb) + (dot(a_low, b_high, ca, cb) + dot(a_high, b_low, ca, cb))


def dot_exact(a, b):
    return lax.dot_general(
        a, b, (((1,), (0,)), ((), ())), precision=HIGHEST, preferred_element_type=F32
    )


def dot_split(a, b):
    high = a.astype(BF16)
    low = (a - high.astype(F32)).astype(BF16)
    return dot(high, b) + dot(low, b)


def rounded(a, parts):
    return a if parts > 1 else a.astype(BF16).astype(F32)


def iota(shape, dim):
    return lax.broadcasted_iota(jnp.int32, shape, dim)


def sigmoid(v):
    return 1.0 / (1.0 + jnp.exp(-v))


def softplus(v):
    return jnp.maximum(v, 0.0) + jnp.log1p(jnp.exp(-jnp.abs(v)))


def column(value, lane):
    return jnp.broadcast_to(value[:, lane : lane + 1], (value.shape[0], LANES))


def pair_lanes(first, second):
    return jnp.where(iota(first.shape, 1) < LANES // 2, first, second)


def earlier(value, tail, steps):
    turned = pltpu.roll(value, steps, 0)
    head = jnp.where(iota(tail.shape, 0) < steps, pltpu.roll(tail, steps, 0), turned[:8])
    return jnp.concatenate([head, turned[8:]], axis=0)


def later(value, following, steps):
    rows = value.shape[0]
    turned = pltpu.roll(value, rows - steps, 0)
    end = jnp.where(
        iota(following.shape, 0) >= 8 - steps,
        pltpu.roll(following, 8 - steps, 0),
        turned[rows - 8 :],
    )
    return jnp.concatenate([turned[: rows - 8], end], axis=0)


def forward_body(
    width, state, taps, per_seq, p_ref, conv_ref, head_ref, lane_ref,
    v_ref, y_ref, u_ref, square_ref, enter_ref, tail, run,
):
    channels = width + 2 * state
    pairs = width // LANES

    @pl.when(pl.program_id(0) % per_seq == 0)
    def _():
        tail[...] = jnp.zeros_like(tail)
        run[...] = jnp.zeros_like(run)

    conv_in = p_ref[:, width : width + channels]
    before = tail[...]
    convolved = conv_ref[taps : taps + 1] + conv_ref[taps - 1 : taps] * conv_in
    for steps in range(1, taps):
        convolved = convolved + conv_ref[taps - 1 - steps : taps - steps] * earlier(
            conv_in, before, steps
        )
    tail[...] = conv_in[L - 8 :]
    v_ref[...] = convolved
    active = convolved * sigmoid(convolved)
    x = active[:, :width]
    write = active[:, width : width + state]
    read = active[:, width + state :]
    step = softplus(p_ref[:, width + channels :] + head_ref[0:1])
    causal = iota((L, L), 0) >= iota((L, L), 1)
    cum = dot_exact(causal.astype(F32), step * head_ref[1:2])
    cum_rows = cum.T
    scores = mm(read, write, 1, 1, PG)
    running = run[...]
    enter_ref[...] = running.astype(enter_ref.dtype)
    carried = mm(read, running, 1, 0, PS)
    first_half = iota((L, LANES), 1) < LANES // 2
    to_state, decays, y_parts = [], [], []
    for q in range(pairs):
        weights, columns = [], []
        for h in (2 * q, 2 * q + 1):
            col = column(cum, h)
            columns.append(col)
            gap = jnp.where(causal, col - cum_rows[h : h + 1], -jnp.inf)
            weights.append(jnp.exp(gap) * scores)
        cum_pair = pair_lanes(*columns)
        step_pair = pair_lanes(column(step, 2 * q), column(step, 2 * q + 1))
        span = slice(q * LANES, (q + 1) * LANES)
        scaled = x[:, span] * step_pair
        inside = mm(
            jnp.concatenate(weights, axis=1),
            jnp.concatenate(
                [jnp.where(first_half, scaled, 0.0), jnp.where(first_half, 0.0, scaled)], axis=0
            ),
            1, 0, PM,
        )
        last = cum_pair[L - 1 :]
        to_state.append(scaled * jnp.exp(last - cum_pair))
        decays.append(jnp.exp(last))
        y_parts.append(inside + jnp.exp(cum_pair) * carried[:, span])
    y = jnp.concatenate(y_parts, axis=1)
    y_ref[...] = y
    run[...] = jnp.concatenate(decays, axis=1) * running + mm(
        write, jnp.concatenate(to_state, axis=1), 0, 0, PS
    )
    gate = p_ref[:, :width]
    mixed = y + lane_ref[0:1] * x
    gated = mixed * (gate * sigmoid(gate))
    u_ref[...] = (gated * lane_ref[1:2]).astype(BF16)
    squares = gated * gated
    total = squares[:, :LANES]
    for q in range(1, pairs):
        total = total + squares[:, q * LANES : (q + 1) * LANES]
    square_ref[...] = total


def backward_body(
    width, state, taps, per_seq, p_ref, v_ref, y_ref, enter_ref, grad_ref, stat_ref,
    conv_ref, head_ref, lane_ref, expand_ref,
    gp_ref, conv_acc, lane_acc, head_acc, ahead, run, leaving,
):
    channels = width + 2 * state
    pairs = width // LANES

    @pl.when(pl.program_id(0) == 0)
    def _():
        conv_acc[...] = jnp.zeros_like(conv_acc)
        lane_acc[...] = jnp.zeros_like(lane_acc)
        head_acc[...] = jnp.zeros_like(head_acc)

    @pl.when(pl.program_id(0) % per_seq == 0)
    def _():
        ahead[...] = jnp.zeros_like(ahead)
        run[...] = jnp.zeros_like(run)
        leaving[...] = jnp.zeros_like(leaving)

    convolved = v_ref[...]
    bend = sigmoid(convolved)
    active = convolved * bend
    slope = bend * (1.0 + convolved * (1.0 - bend))
    x = active[:, :width]
    write = active[:, width : width + state]
    read = active[:, width + state :]
    raw = p_ref[:, width + channels :] + head_ref[0:1]
    rate = head_ref[1:2]
    step = softplus(raw)
    log_decay = step * rate
    upper = iota((L, L), 0) <= iota((L, L), 1)
    lower = iota((L, L), 0) >= iota((L, L), 1)
    cum = dot_exact(lower.astype(F32), log_decay)
    cum_rows = cum.T

    gate = p_ref[:, :width]
    y = y_ref[...]
    grad = grad_ref[...]
    gate_bend = sigmoid(gate)
    gate_silu = gate * gate_bend
    mixed = y + lane_ref[0:1] * x
    gated = mixed * gate_silu
    inverse = jnp.broadcast_to(stat_ref[:, 0:1], (L, width))
    pull = jnp.broadcast_to(stat_ref[:, 1:2], (L, width))
    scaled_grad = inverse * grad
    grad_gated = scaled_grad * lane_ref[1:2] - gated * pull
    gp_ref[:, :width] = (
        grad_gated * mixed * (gate_bend * (1.0 + gate * (1.0 - gate_bend)))
    ).astype(BF16)
    grad_y = grad_gated * gate_silu
    lane_acc[0:1] += jnp.sum(scaled_grad * gated, axis=0, keepdims=True)
    lane_acc[1:2] += jnp.sum(grad_y * x, axis=0, keepdims=True)
    grad_low = rounded(grad_y, PM)

    scores = mm(write, read, 1, 1, PG)
    grad_state = run[...]
    from_state = mm(write, grad_state, 1, 0, PS)
    entering = enter_ref[...]
    first_half = iota((L, LANES), 1) < LANES // 2
    grad_scores = jnp.zeros((L, L), F32)
    to_state, grad_carried, decays, grad_scaled, lows, steps = [], [], [], [], [], []
    for q in range(pairs):
        span = slice(q * LANES, (q + 1) * LANES)
        step_pair = pair_lanes(column(step, 2 * q), column(step, 2 * q + 1))
        scaled = x[:, span] * step_pair
        low = rounded(scaled, PM)
        dy = grad_low[:, span]
        outer = mm(
            jnp.concatenate(
                [jnp.where(first_half, low, 0.0), jnp.where(first_half, 0.0, low)], axis=0
            ),
            dy,
            1,
            1,
            PO,
        )
        weights, columns = [], []
        for k in range(2):
            h = 2 * q + k
            col = column(cum, h)
            columns.append(col)
            decay = jnp.exp(jnp.where(upper, cum_rows[h : h + 1] - col, -jnp.inf))
            weights.append(decay * scores)
            grad_scores = grad_scores + decay * outer[k * L : (k + 1) * L]
        inside = mm(
            jnp.concatenate(weights, axis=1),
            jnp.concatenate(
                [jnp.where(first_half, dy, 0.0), jnp.where(first_half, 0.0, dy)], axis=0
            ),
            1,
            0,
            PM,
        )
        cum_pair = pair_lanes(*columns)
        last = cum_pair[L - 1 :]
        to_end = jnp.exp(last - cum_pair)
        to_state.append(scaled * to_end)
        grad_carried.append(grad_y[:, span] * jnp.exp(cum_pair))
        decays.append(jnp.exp(last))
        grad_scaled.append(inside + to_end * from_state[:, span])
        lows.append(low)
        steps.append(step_pair)
    grad_scaled = jnp.concatenate(grad_scaled, axis=1)
    to_state = jnp.concatenate(to_state, axis=1)
    grad_carried = jnp.concatenate(grad_carried, axis=1)
    lows = jnp.concatenate(lows, axis=1)
    steps = jnp.concatenate(steps, axis=1)
    grad_write = mm(grad_scores, read, 1, 0, PO) + mm(to_state, grad_state, 1, 1, PC)
    grad_read = mm(grad_scores, write, 0, 0, PO) + mm(grad_carried, entering, 1, 1, PC)
    across = jnp.sum(leaving[...].astype(F32) * grad_state, axis=0, keepdims=True)
    run[...] = jnp.concatenate(decays, axis=1) * grad_state + mm(read, grad_carried, 0, 0, PS)
    leaving[...] = entering

    rows = jnp.concatenate(
        [
            y * grad_low - lows * grad_scaled,
            x * grad_scaled,
            jnp.broadcast_to(across, (8, width)),
        ],
        axis=0,
    )
    by_head = dot_split(rows, expand_ref[...])
    grad_decay = dot_split_left(upper.astype(BF16), by_head[:L]) + by_head[2 * L : 2 * L + 1]
    grad_step = by_head[L : 2 * L] + rate * grad_decay
    grad_raw = grad_step * sigmoid(raw)
    head_acc[0:1] += jnp.sum(grad_raw, axis=0, keepdims=True)
    head_acc[1:2] += jnp.sum(grad_decay * log_decay, axis=0, keepdims=True)
    gp_ref[:, width + channels :] = grad_raw.astype(BF16)

    grad_x = grad_scaled * steps + lane_ref[0:1] * grad_y
    grad_conv = jnp.concatenate([grad_x, grad_write, grad_read], axis=1) * slope
    following = ahead[...]
    conv_in = p_ref[:, width : width + channels]
    total = conv_ref[taps - 1 : taps] * grad_conv
    conv_acc[taps - 1 : taps] += jnp.sum(grad_conv * conv_in, axis=0, keepdims=True)
    conv_acc[taps : taps + 1] += jnp.sum(grad_conv, axis=0, keepdims=True)
    for steps_on in range(1, taps):
        moved = later(grad_conv, following, steps_on)
        row = taps - 1 - steps_on
        total = total + conv_ref[row : row + 1] * moved
        conv_acc[row : row + 1] += jnp.sum(moved * conv_in, axis=0, keepdims=True)
    ahead[...] = grad_conv[:8]
    gp_ref[:, width : width + channels] = total.astype(BF16)


def dot_split_left(a, b):
    high = b.astype(BF16)
    low = (b - high.astype(F32)).astype(BF16)
    return dot(a, high) + dot(a, low)


def forward_scan(projected, conv_rows, head_rows, lane_rows, width, state, taps, per_seq):
    tokens, columns = projected.shape
    blocks = tokens // L
    channels = width + 2 * state
    whole = lambda i: (0, 0)
    mine = lambda i: (i, 0)
    return pl.pallas_call(
        functools.partial(forward_body, width, state, taps, per_seq),
        grid=(blocks,),
        in_specs=[
            pl.BlockSpec((L, columns), mine),
            pl.BlockSpec(conv_rows.shape, whole),
            pl.BlockSpec(head_rows.shape, whole),
            pl.BlockSpec(lane_rows.shape, whole),
        ],
        out_specs=[
            pl.BlockSpec((L, channels), mine),
            pl.BlockSpec((L, width), mine),
            pl.BlockSpec((L, width), mine),
            pl.BlockSpec((L, LANES), mine),
            pl.BlockSpec((state, width), mine),
        ],
        out_shape=[
            jax.ShapeDtypeStruct((tokens, channels), F32),
            jax.ShapeDtypeStruct((tokens, width), F32),
            jax.ShapeDtypeStruct((tokens, width), BF16),
            jax.ShapeDtypeStruct((tokens, LANES), F32),
            jax.ShapeDtypeStruct((blocks * state, width), ENTER),
        ],
        scratch_shapes=[pltpu.VMEM((8, channels), F32), pltpu.VMEM((state, width), F32)],
        compiler_params=pltpu.CompilerParams(
            dimension_semantics=("arbitrary",), vmem_limit_bytes=VMEM_LIMIT
        ),
        cost_estimate=pl.CostEstimate(
            flops=tokens * width * 1024, bytes_accessed=tokens * columns * 10, transcendentals=0
        ),
        name="forward_scan",
    )(projected, conv_rows, head_rows, lane_rows)


def backward_scan(
    projected, convolved, y, entering, grad, stats, conv_rows, head_rows, lane_rows, expand,
    width, state, taps, per_seq,
):
    tokens, columns = projected.shape
    blocks = tokens // L
    channels = width + 2 * state
    whole = lambda i: (0, 0)
    mine = lambda i: (blocks - 1 - i, 0)
    return pl.pallas_call(
        functools.partial(backward_body, width, state, taps, per_seq),
        grid=(blocks,),
        in_specs=[
            pl.BlockSpec((L, columns), mine),
            pl.BlockSpec((L, channels), mine),
            pl.BlockSpec((L, width), mine),
            pl.BlockSpec((state, width), mine),
            pl.BlockSpec((L, width), mine),
            pl.BlockSpec((L, stats.shape[1]), mine),
            pl.BlockSpec(conv_rows.shape, whole),
            pl.BlockSpec(head_rows.shape, whole),
            pl.BlockSpec(lane_rows.shape, whole),
            pl.BlockSpec(expand.shape, whole),
        ],
        out_specs=[
            pl.BlockSpec((L, columns), mine),
            pl.BlockSpec(conv_rows.shape, whole),
            pl.BlockSpec(lane_rows.shape, whole),
            pl.BlockSpec(head_rows.shape, whole),
        ],
        out_shape=[
            jax.ShapeDtypeStruct((tokens, columns), BF16),
            jax.ShapeDtypeStruct(conv_rows.shape, F32),
            jax.ShapeDtypeStruct(lane_rows.shape, F32),
            jax.ShapeDtypeStruct(head_rows.shape, F32),
        ],
        scratch_shapes=[
            pltpu.VMEM((8, channels), F32),
            pltpu.VMEM((state, width), F32),
            pltpu.VMEM((state, width), ENTER),
        ],
        compiler_params=pltpu.CompilerParams(
            dimension_semantics=("arbitrary",), vmem_limit_bytes=VMEM_LIMIT
        ),
        cost_estimate=pl.CostEstimate(
            flops=tokens * width * 3072, bytes_accessed=tokens * columns * 14, transcendentals=0
        ),
        name="backward_scan",
    )(projected, convolved, y, entering, grad, stats, conv_rows, head_rows, lane_rows, expand)


def rows_of(vectors, lanes):
    made = [jnp.pad(v.astype(F32), ((0, 0), (0, lanes - v.shape[1]))) for v in vectors]
    stacked = jnp.concatenate(made, axis=0)
    return jnp.pad(stacked, ((0, 8 - stacked.shape[0]), (0, 0)))


def send(value, sizes, move):
    nb, ns = sizes
    pairs = []
    for b in range(nb):
        for s in range(ns):
            goal = move(b, s)
            if goal is not None:
                pairs.append((b * ns + s, goal[0] * ns + goal[1]))
    return lax.ppermute(value, AXES, pairs)


def swap_core(value, sizes):
    return send(value, sizes, lambda b, s: (b, s ^ 1))


def turn_row(value, sizes, k):
    return send(value, sizes, lambda b, s: (b, (s + 2 * k) % sizes[1]))


def scatter_pieces(value, sizes):
    ns = sizes[1]
    me = lax.axis_index("seq")
    chip, core = me // 2, me % 2
    split = value.reshape((ns // 2, 2) + value.shape[1:])
    give = lax.dynamic_index_in_dim(split, 1 - core, 1, False).astype(BF16)
    keep = lax.dynamic_index_in_dim(split, core, 1, False)
    both = keep + swap_core(give, sizes).astype(F32)
    total = lax.dynamic_index_in_dim(both, chip, 0, False)
    for k in range(1, ns // 2):
        part = lax.dynamic_index_in_dim(both, (chip + k) % (ns // 2), 0, False)
        part = turn_row(part.astype(BF16), sizes, k)
        total = total + part.astype(F32)
    return total


def add_over(value, sizes, axis):
    k = 1
    while k < sizes[axis]:
        step = k
        if axis == 0:
            other = send(value, sizes, lambda b, s: (b ^ step, s))
        else:
            other = send(value, sizes, lambda b, s: (b, s ^ step))
        value = value + other
        k *= 2
    return value


def sum_depth(value, sizes):
    deep = sizes[0] // 2
    z = lax.axis_index("batch") // 2
    got = [value]
    for k in range(1, deep):
        got.append(turn_deep(value, sizes, k))
    got = jnp.stack(got)
    at = lambda d: lax.dynamic_index_in_dim(got, (z + deep - d) % deep, 0, False)
    return functools.reduce(jnp.add, [at(d) for d in range(deep)])


def sum_seq(value, sizes):
    total = value
    for k in range(1, sizes[1]):
        other = turn_seq(value, sizes, k)
        total = total + other
    return total


def collect(value, index, count, sizes, axes):
    total = lax.dynamic_update_index_in_dim(
        jnp.zeros((count,) + value.shape, value.dtype), value, index, 0
    )
    for axis in axes:
        total = add_over(total, sizes, axis)
    return total


def after(value, other):
    return lax.optimization_barrier((value, other))[0]


def swap_side(value, sizes):
    return send(value, sizes, lambda b, s: (b ^ 1, s))


def turn_deep(value, sizes, k):
    deep = sizes[0] // 2
    return send(value, sizes, lambda b, s: ((b // 2 + k) % deep * 2 + b % 2, s))


def turn_seq(value, sizes, k):
    return send(value, sizes, lambda b, s: (b, (s + k) % sizes[1]))


def exchange_seq(blocks, sizes):
    ns = sizes[1]
    me = lax.axis_index("seq")
    total = lax.dynamic_update_index_in_dim(
        jnp.zeros_like(blocks), lax.dynamic_index_in_dim(blocks, me, 0, False), me, 0
    )
    for k in range(1, ns):
        part = lax.dynamic_index_in_dim(blocks, (me + k) % ns, 0, False)
        got = turn_seq(part, sizes, k)
        total = lax.dynamic_update_index_in_dim(total, got, (me + ns - k) % ns, 0)
    return total


def gather_batch(block, sizes):
    deep = sizes[0] // 2
    me = lax.axis_index("batch")
    z, x = me // 2, me % 2
    total = jnp.zeros((deep * 2,) + block.shape, block.dtype)
    place = lambda part, at: lax.dynamic_update_index_in_dim(total, part, at, 0)
    here = block
    for k in range(deep):
        there = swap_side(here, sizes)
        at = (z + deep - k) % deep * 2
        total = place(here, at + x)
        if k < deep - 1:
            here = turn_deep(here, sizes, 1)
        total = place(there, at + 1 - x)
    return total.reshape((-1,) + block.shape[1:]), here


def sides(blocks, sizes):
    x = lax.axis_index("batch") % 2
    split = blocks.reshape((sizes[0] // 2, 2) + blocks.shape[1:])
    pick = lambda side: lax.dynamic_index_in_dim(split, side, 1, False)
    return pick(1 - x), pick(x)


def scatter_batch(blocks, sizes):
    deep = sizes[0] // 2
    z = lax.axis_index("batch") // 2
    give, keep = sides(blocks, sizes)
    pick = lambda value, at: lax.dynamic_index_in_dim(value, at % deep, 0, False)
    total = None
    for k in range(1, deep + 1):
        at = z + deep - k
        other = swap_side(pick(give, at), sizes)
        both = pick(keep, at).astype(F32) + other.astype(F32)
        total = both if total is None else total + both
        if k < deep:
            total = turn_deep(total.astype(BF16), sizes, 1)
            total = total.astype(F32)
    return total


def per_device(
    sizes, hidden, in_proj, out_proj, conv_weight, conv_bias, step_bias, decay_log,
    skip_weight, gated_gain, norm_gain, cotangent,
):
    nb, ns = sizes
    devices = nb * ns
    me_b, me_s = lax.axis_index("batch"), lax.axis_index("seq")
    seq_count, piece, model = hidden.shape
    taps, conv_part = conv_weight.shape
    conv_channels = conv_part * devices
    inner = out_proj.shape[0] * devices
    heads = step_bias.shape[0]
    state = (conv_channels - inner) // 2
    in_rows = in_proj.shape[0]
    own_heads = heads // ns
    width = inner // ns
    head_size = inner // heads
    channels = width + 2 * state
    columns = width + channels + LANES
    tokens = seq_count * piece * ns
    per_seq = piece * ns // L

    dt_at = inner + conv_channels
    small = jnp.concatenate([conv_weight.reshape(-1), conv_bias, gated_gain])
    small_count = small.shape[0]
    small_lanes = -(-small_count // in_rows)
    small = jnp.pad(small, (0, small_lanes * in_rows - small_count)).reshape(in_rows, small_lanes)
    spare = LANES - own_heads - small_lanes
    payload = jnp.stack(
        [
            jnp.concatenate(
                [
                    in_proj[:, s * width : (s + 1) * width],
                    in_proj[:, inner + s * width : inner + (s + 1) * width],
                    in_proj[:, 2 * inner : dt_at],
                    in_proj[:, dt_at + s * own_heads : dt_at + (s + 1) * own_heads],
                    small,
                    jnp.zeros((in_rows, spare), BF16),
                ],
                axis=1,
            )
            for s in range(ns)
        ]
    )
    gains = after(jnp.pad(norm_gain.astype(F32), (0, -in_rows % LANES)), payload)
    gains = collect(gains, me_b * ns + me_s, devices, sizes, (0, 1))
    norm_all = gains[:, :in_rows].reshape(1, model)
    mine = exchange_seq(payload, sizes).reshape(ns * in_rows, columns)
    weight_in, last_in = gather_batch(mine, sizes)
    out_rows = lax.ppermute(
        after(out_proj, mine), AXES, [(j, (j % nb) * ns + j // nb) for j in range(devices)]
    )

    at = width + channels + own_heads
    small = weight_in[:, at : at + small_lanes].astype(F32).reshape(devices, -1)
    conv_all = jnp.moveaxis(
        small[:, : taps * conv_part].reshape(devices, taps, conv_part), 0, 1
    ).reshape(taps, conv_channels)
    at = taps * conv_part
    bias_all = small[:, at : at + conv_part].reshape(1, conv_channels)
    at += conv_part
    gain_all = small[:, at : at + gated_gain.shape[0]].reshape(1, inner)
    conv_all = jnp.concatenate([conv_all, bias_all], axis=0)
    conv_rows = rows_of(
        [
            jnp.concatenate(
                [
                    lax.dynamic_slice_in_dim(conv_all, me_s * width, width, 1),
                    conv_all[:, inner:],
                ],
                axis=1,
            )
        ],
        channels,
    )
    own = lambda v: lax.dynamic_slice_in_dim(v, me_s * own_heads, own_heads, 0)
    head_rows = rows_of([own(step_bias)[None], -jnp.exp(own(decay_log))[None]], LANES)
    lane_rows = rows_of(
        [
            jnp.repeat(own(skip_weight), head_size)[None],
            lax.dynamic_slice_in_dim(gain_all, me_s * width, width, 1),
        ],
        width,
    )
    expand = (
        jnp.arange(width)[:, None] // head_size == jnp.arange(LANES)[None, :]
    ).astype(BF16)

    def in_order(pieces):
        value = pieces.reshape((ns, seq_count, piece, model))
        return jnp.swapaxes(value, 0, 1).reshape(tokens, model)

    def in_pieces(value):
        value = value.reshape((seq_count, ns, piece, model))
        return jnp.swapaxes(value, 0, 1).reshape(ns, seq_count * piece, model)

    low = hidden.reshape(-1, model)
    grad_low = cotangent.reshape(-1, model)
    hidden_all = after(in_order(lax.all_gather(low, "seq")), last_in).astype(F32)
    spread = lax.rsqrt(jnp.mean(hidden_all * hidden_all, axis=-1, keepdims=True) + EPSILON)
    normed_all = (hidden_all * spread * norm_all).astype(BF16)
    upstream = lax.all_gather(after(grad_low, payload), "seq")
    upstream = in_order(upstream)
    weight_out = lax.all_gather(out_rows, "batch", axis=0, tiled=True)

    projected = jnp.dot(normed_all, weight_in, preferred_element_type=F32)
    convolved, y, ungained, squares, entering = forward_scan(
        projected, conv_rows, head_rows, lane_rows, width, state, taps, per_seq
    )
    weight_out = after(weight_out, ungained)
    grad_gated = jnp.einsum("td,kd->tk", upstream, weight_out, preferred_element_type=F32)
    sums = jnp.stack(
        [
            jnp.sum(squares, axis=1),
            jnp.sum(grad_gated * ungained.astype(F32), axis=1),
        ]
    )
    sums = sum_seq(sums, sizes)
    inverse = lax.rsqrt(sums[0] / inner + EPSILON)
    pull = inverse * inverse * inverse * sums[1] / inner
    stats = jnp.stack([inverse, pull], axis=1)
    out_partial = jnp.dot(ungained, weight_out, preferred_element_type=F32)
    out_sum = scatter_pieces(in_pieces(out_partial), sizes)
    own_inverse = lax.dynamic_index_in_dim(
        jnp.swapaxes(inverse.reshape(seq_count, ns, piece), 0, 1), me_s, 0, False
    ).reshape(-1, 1)
    stream = low.astype(F32)
    result = (stream + own_inverse * out_sum).astype(BF16)
    gated_low = (ungained.astype(F32) * inverse[:, None]).astype(BF16)
    grad_out_w = jnp.einsum("tk,td->kd", gated_low, upstream, preferred_element_type=F32)

    grad_proj, conv_acc, lane_acc, head_acc = backward_scan(
        projected, convolved, y, entering, grad_gated, after(stats, grad_out_w), conv_rows, head_rows, lane_rows,
        expand, width, state, taps, per_seq,
    )
    cut = (columns // 2 + LANES - 1) // LANES * LANES
    grad_in_w = []
    for name, lo, hi in (("a", 0, cut), ("b", cut, columns)):
        part = jnp.einsum("td,tk->dk", normed_all, grad_proj[:, lo:hi], preferred_element_type=F32)
        grad_in_w.append((name, part.astype(BF16).reshape(nb, ns * in_rows, hi - lo)))
    scaled = jnp.einsum("tk,dk->td", grad_proj, weight_in, preferred_element_type=F32)
    scaled = lax.psum_scatter(
        in_pieces(scaled.astype(BF16)), "seq", scatter_dimension=0, tiled=False
    ).astype(F32) * norm_all
    own_spread = lax.rsqrt(jnp.mean(stream * stream, axis=-1, keepdims=True) + EPSILON)
    unit = stream * own_spread
    grad_stream = own_spread * (scaled - unit * jnp.mean(scaled * unit, axis=-1, keepdims=True))
    hidden_grad = (grad_low.astype(F32) + grad_stream).astype(BF16)

    out_part = lax.psum_scatter(
        grad_out_w.astype(BF16), "batch", scatter_dimension=0, tiled=True
    )
    out_proj_grad = lax.ppermute(
        out_part, AXES, [((j % nb) * ns + j // nb, j) for j in range(devices)]
    ).astype(F32)
    by_source = []
    for name, part in grad_in_w:
        part = scatter_batch(part, sizes).astype(BF16)
        by_source.append(exchange_seq(part.reshape(ns, in_rows, -1), sizes))
    by_source = jnp.concatenate(by_source, axis=2).astype(F32)
    across = lambda lo, hi: jnp.concatenate([by_source[s, :, lo:hi] for s in range(ns)], axis=1)
    in_proj_grad = jnp.concatenate(
        [
            across(0, width),
            across(width, 2 * width),
            jnp.sum(by_source[:, :, 2 * width : width + channels], axis=0),
            across(width + channels, width + channels + own_heads),
        ],
        axis=1,
    )
    norm_gain_grad = jnp.sum(in_proj.astype(F32) * in_proj_grad, axis=1) / norm_gain.astype(F32)

    by_head = jnp.sum(lane_acc[1].reshape(own_heads, head_size), axis=1)
    packed = jnp.concatenate(
        [
            conv_acc[: taps + 1].reshape(-1),
            lane_acc[0],
            by_head,
            head_acc[0, :own_heads],
            head_acc[1, :own_heads],
        ]
    )
    packed = jnp.pad(packed, (0, -packed.shape[0] % (8 * LANES))).reshape(-1, LANES)
    other = swap_side(packed, sizes)
    packed = packed + other
    packed = sum_depth(packed, sizes)
    packed = collect(packed, me_s, ns, sizes, (1,))
    packed = packed.reshape(ns, -1)
    rows = (taps + 1) * channels
    conv_grads = packed[:, :rows].reshape(ns, taps + 1, channels)
    conv_grads = jnp.concatenate(
        [
            jnp.moveaxis(conv_grads[:, :, :width], 0, 1).reshape(taps + 1, inner),
            jnp.sum(conv_grads[:, :, width:], axis=0),
        ],
        axis=1,
    )
    me = me_b * ns + me_s
    conv_grads = lax.dynamic_slice_in_dim(conv_grads, me * conv_part, conv_part, 1)
    gain_grad = lax.dynamic_slice_in_dim(
        packed[:, rows : rows + width].reshape(-1), me * gated_gain.shape[0], gated_gain.shape[0], 0
    )
    at = rows + width
    skip_grad, bias_grad, rate_grad = (
        packed[:, at + k * own_heads : at + (k + 1) * own_heads].reshape(-1) for k in range(3)
    )
    return (
        result.reshape(hidden.shape),
        hidden_grad.reshape(hidden.shape),
        in_proj_grad,
        out_proj_grad,
        conv_grads[:taps],
        conv_grads[taps],
        bias_grad,
        rate_grad,
        skip_grad,
        gain_grad,
        norm_gain_grad,
    )


def solution(mesh):
    both = P(AXES)
    in_specs = (
        P("batch", "seq", None),
        P(AXES, None),
        P(AXES, None),
        P(None, AXES),
        both,
        P(),
        P(),
        P(),
        both,
        both,
        P("batch", "seq", None),
    )
    out_specs = (
        P("batch", "seq", None),
        P("batch", "seq", None),
        P(AXES, None),
        P(AXES, None),
        P(None, AXES),
        both,
        P(),
        P(),
        P(),
        both,
        both,
    )
    sizes = (mesh.shape["batch"], mesh.shape["seq"])

    def step(*args):
        return per_device(sizes, *args)

    return jax.shard_map(
        step, mesh=mesh, in_specs=in_specs, out_specs=out_specs, check_vma=False
    )
```
